32 devices in a mesh: band: 8 (over z, y), grid: 4 (over x, core).
Axes of the slice: x: 2, y: 2, z: 4, core: 2. Of those that a mesh axis runs over, the one named last changes fastest.
Arguments:
- x_initial: float32 [160, 3, 256, 256], P(('band', 'grid')), may hold values from -0.1 to 1, as said below
- sp2_choices: int32 [4], replicated, may hold values from 0 to 1, as said below
- domain_blocks: int32 [96, 5], replicated, may hold values from -1 to 159, as said below
- basis_values: bfloat16 [96, 768, 1280], P(('band', 'grid')), may hold values from -0.25 to 0.25
Outputs:
- density: float32 [160, 3, 256, 256], P(('band', 'grid'))
- hamiltonian: float32 [160, 3, 256, 256], P(('band', 'grid'))
- potential: float32 [96, 768], P(('band', 'grid'))
The draws below stay inside these ranges and needn't reach their ends.
Inputs may be any that keep to these rules, and one draw needn't show every extreme that they name: Lower block form of a symmetric matrix: each x_initial[I, 2] is symmetric, and the blocks x_initial[I, q] with I - 2 + q < 0 are zero. `domain_blocks`: domain rows are grouped by device in the order of the joined axes band then grid, 3 rows a device. A row lists 2 to 5 consecutive block numbers followed by -1 entries. All blocks of a domain are block rows of one device with the same grid index whose band index differs from the domain's device by at most 2; the domains of one device lie on different devices. Every device has a domain of 5 blocks. `sp2_choices`: not all steps apply the same polynomial.
All inputs are finite; a program needn't handle non-finite values.
Results may differ from the reference program's by a relative error of at most 0.0017.
The reference program's roundings to bfloat16 on the way count: a program that leaves them out, or rounds other values in their place, can miss the bound.
Values may be sent and summed in bfloat16 or wider, within the bound.
A program may use at most 128 MiB of HBM per device.

```python
import jax
import jax.numpy as jnp
from jax import lax

BS = 256
DBLK = 5
NPT = 768
RB = 5
DOM = 3
REACH = 2
ITERS = 4
DOMAINS = 96
N_BAND = 8
N_GRID = 4


def draw_sp2_choices(key, part):
    values = jax.random.randint(jax.random.fold_in(key, 7), (ITERS,), 0, 2).astype(jnp.int32)
    alike = jnp.all(values == values[0])
    last_value = jnp.where(alike, 1 - values[ITERS - 1], values[ITERS - 1]).astype(jnp.int32)
    return values.at[ITERS - 1].set(last_value).astype(jnp.int32)


def draw_x_initial(key, part):
    row_total = RB * N_BAND * N_GRID
    key_level, key_noise = jax.random.split(key)
    levels = jax.random.uniform(key_level, (row_total, BS), jnp.float32, 0.2, 0.8)
    noise_blocks = 0.004 * jax.random.normal(key_noise, (row_total, 3, BS, BS), jnp.float32)
    diagonal = 0.5 * (noise_blocks[:, 2] + jnp.swapaxes(noise_blocks[:, 2], 1, 2))
    identity_matrix = jnp.eye(BS, dtype=jnp.float32)
    diagonal = diagonal + levels[:, :, None] * identity_matrix[None]
    lower_blocks = jnp.concatenate([noise_blocks[:, :2], diagonal[:, None]], axis=1)
    row_index = jnp.arange(row_total, dtype=jnp.int32)[:, None]
    slot_index = jnp.arange(3, dtype=jnp.int32)[None, :]
    present = (row_index - 2 + slot_index >= 0).astype(jnp.float32)
    return lower_blocks * present[:, :, None, None]


def draw_domain_blocks(key, part):
    device_total = N_BAND * N_GRID
    slot_total = 2 * REACH + 1
    key_order, key_count, key_full, key_place = jax.random.split(key, 4)
    device_ids = jnp.arange(device_total, dtype=jnp.int32)
    band_ids = device_ids // N_GRID
    grid_ids = device_ids % N_GRID
    band_moves = jnp.arange(slot_total, dtype=jnp.int32) - REACH
    target_band = band_ids[:, None] + band_moves[None, :]
    allowed = (target_band >= 0) & (target_band < N_BAND)
    scores = jax.random.randint(key_order, (device_total, slot_total), 0, 1024) * 16 + jnp.arange(slot_total, dtype=jnp.int32)[None, :]
    scores = jnp.where(allowed, scores, 1 << 20)
    ranking = jnp.argsort(scores, axis=1, stable=True)[:, :DOM]
    chosen_band = jnp.take_along_axis(target_band, ranking, axis=1)
    owners = chosen_band * N_GRID + grid_ids[:, None]
    counts = jax.random.randint(key_count, (device_total, DOM), 2, DBLK + 1)
    full_slot = jax.random.randint(key_full, (device_total, 1), 0, DOM)
    counts = jnp.where(jnp.arange(DOM, dtype=jnp.int32)[None, :] == full_slot, DBLK, counts)
    offset_rows = jax.random.randint(key_place, (device_total, DOM), 0, 1 << 20) % (RB - counts + 1)
    first_block = owners * RB + offset_rows
    positions = jnp.arange(DBLK, dtype=jnp.int32)
    block_ids = jnp.where(positions[None, None, :] < counts[:, :, None], first_block[:, :, None] + positions[None, None, :], -1)
    return block_ids.reshape(device_total * DOM, DBLK).astype(jnp.int32)


def steps_of(key, extent, cuts, low, top_value):
    def one(position, blocks):
        draws = jax.random.uniform(jax.random.fold_in(jax.random.fold_in(key, 6), position), (blocks,), jnp.float32, low / len(cuts), top_value / len(cuts))
        return jnp.repeat(jnp.exp(draws), extent[position] // blocks).reshape((-1,) + (1,) * (len(extent) - position - 1))

    gain = one(*cuts[0])
    for cut in cuts[1:]:
        gain = gain * one(*cut)
    return gain


def bell_draw(stream_key, dims, deviation, reach, cuts=(), held_as=jnp.bfloat16):
    factor_of = steps_of(stream_key, dims, cuts, -0.22, 0.18) if cuts else 1.0
    drawn = jax.random.normal(stream_key, dims, jnp.float32) * deviation * factor_of
    return jnp.minimum(jnp.maximum(drawn, -reach), reach).astype(held_as)


def setup_inputs(seed: int = 0) -> dict:
    arg_keys = jax.random.split(jax.random.key(seed), 5)
    return {
        "x_initial": draw_x_initial(jax.random.fold_in(arg_keys[4], 71), 0),
        "sp2_choices": draw_sp2_choices(jax.random.fold_in(arg_keys[4], 71), 0),
        "domain_blocks": draw_domain_blocks(jax.random.fold_in(arg_keys[4], 71), 0),
        "basis_values": bell_draw(arg_keys[3], (DOMAINS, NPT, DBLK * BS), (DBLK * BS // 2) ** -0.5, 0.25, ((0, 32),)),
    }


HIGHEST_PRECISION = lax.Precision.HIGHEST


def pair_product(left_block, right_block, left_turned, right_turned):
    pattern = ("rba" if left_turned else "rab") + "," + ("rcb" if right_turned else "rbc") + "->rac"
    return jnp.einsum(pattern, left_block, right_block, precision=HIGHEST_PRECISION)


def square_lower(padded, row_count):
    results = []
    for diag_gap in range(3):
        summed = jnp.zeros((row_count,) + padded.shape[2:], jnp.float32)
        for middle_gap in range(-2, 3 - diag_gap):
            if middle_gap <= 0:
                left_block = padded[2:2 + row_count, 2 + middle_gap]
                left_turned = False
            else:
                left_block = padded[2 + middle_gap:2 + middle_gap + row_count, 2 - middle_gap]
                left_turned = True
            outer_gap = middle_gap + diag_gap
            if outer_gap >= 0:
                right_block = padded[2 + middle_gap:2 + middle_gap + row_count, 2 - outer_gap]
                right_turned = False
            else:
                right_block = padded[2 - diag_gap:2 - diag_gap + row_count, 2 + outer_gap]
                right_turned = True
            summed = summed + pair_product(left_block, right_block, left_turned, right_turned)
        results.append(summed)
    return jnp.stack([results[2], results[1], results[0]], axis=1)


def domain_terms(basis_row, density_tile, block_count):
    points = basis_row.shape[0]
    blocks_here = density_tile.shape[0]
    block_width = density_tile.shape[2]
    live_mask = (jnp.arange(blocks_here) < block_count).astype(basis_row.dtype)
    shaped = basis_row.reshape(points, blocks_here, block_width) * live_mask[None, :, None]
    shaped_wide = shaped.astype(jnp.float32)
    tile_wide = density_tile.astype(jnp.float32)
    density = jnp.zeros((points,), jnp.float32)
    for diag_gap in range(3):
        weight = 1.0 if diag_gap == 0 else 2.0
        applied = jnp.einsum("pkb,kbc->pkc", shaped_wide[:, diag_gap:], tile_wide[diag_gap:, 2 - diag_gap], precision=HIGHEST_PRECISION)
        density = density + weight * jnp.sum(applied * shaped_wide[:, :blocks_here - diag_gap], axis=(1, 2))
    potential = jnp.tanh(density)
    factor = blocks_here * block_width / points
    scaled = ((factor * potential)[:, None, None] * shaped_wide).astype(jnp.bfloat16)
    scaled = lax.optimization_barrier(scaled).astype(jnp.float32)
    pieces = []
    for diag_gap in range(3):
        block_sum = jnp.einsum("pkb,pkc->kbc", scaled[:, diag_gap:], shaped_wide[:, :blocks_here - diag_gap], precision=HIGHEST_PRECISION)
        filler = jnp.zeros((diag_gap, block_width, block_width), jnp.float32)
        pieces.append(jnp.concatenate([filler, block_sum], axis=0))
    return potential, jnp.stack([pieces[2], pieces[1], pieces[0]], axis=1)


def reference(x_initial, sp2_choices, domain_blocks, basis_values):
    row_total = x_initial.shape[0]
    lower_band = x_initial
    for iteration in range(ITERS):
        narrow = lax.optimization_barrier(lower_band.astype(jnp.bfloat16))
        padded = jnp.pad(narrow.astype(jnp.float32), ((2, 2), (0, 0), (0, 0), (0, 0)))
        squared = square_lower(padded, row_total)
        lower_band = jnp.where(sp2_choices[iteration] == 1, 2.0 * lower_band - squared, squared)
    rounded = lax.optimization_barrier(lower_band.astype(jnp.bfloat16))
    tile_source = jnp.pad(rounded, ((0, DBLK), (0, 0), (0, 0), (0, 0)))
    counts = jnp.sum((domain_blocks >= 0).astype(jnp.int32), axis=1).astype(jnp.int32)
    starts = domain_blocks[:, 0].astype(jnp.int32)

    def visit_domain(hamiltonian, domain_item):
        first_block, block_count, basis_row = domain_item
        density_tile = lax.dynamic_slice_in_dim(tile_source, first_block, DBLK, 0)
        potential, partial_value = domain_terms(basis_row, density_tile, block_count)
        current = lax.dynamic_slice_in_dim(hamiltonian, first_block, DBLK, 0)
        hamiltonian = lax.dynamic_update_slice_in_dim(hamiltonian, current + partial_value, first_block, 0)
        return hamiltonian, potential

    initial_sum = jnp.zeros((row_total + DBLK,) + lower_band.shape[1:], jnp.float32)
    hamiltonian, potentials = lax.scan(visit_domain, initial_sum, (starts, counts, basis_values))
    return lower_band, hamiltonian[:row_total], potentials
```

```python
import functools

import jax
import jax.numpy as jnp
from jax import lax
from jax.experimental import pallas as pl
from jax.experimental.pallas import tpu as pltpu
from jax.sharding import PartitionSpec as P

REACH = 2
ITERS = 4
SEND_POINTS = 64
PART_POINTS = 256
EDGE_STEP = ITERS - 2
STEP_HOPS = 3
VMEM_LIMIT = 46000000
MESH = pl.DeviceIdType.MESH
F32 = jnp.float32
BF16 = jnp.bfloat16


def product(left, right, left_turned, right_turned):
    dims = (((0 if left_turned else 1,), (1 if right_turned else 0,)), ((), ()))
    return lax.dot_general(left, right, dims, preferred_element_type=F32)


def kernel(
    band_count,
    grid_count,
    blocks_ref,
    choices_ref,
    x_hbm,
    basis_hbm,
    x,
    ham,
    potential_ref,
    basis,
    narrow,
    tiles,
    above,
    below,
    packed,
    arrived,
    transit,
    psi,
    pot_in,
    pot_out,
    local_sem,
    basis_sem,
    halo_send,
    halo_recv,
    basis_send,
    basis_recv,
    hop_send,
    hop_recv,
    pot_send,
    pot_recv,
):
    rows, _, width, _ = x.shape
    _, points, _ = basis_hbm.shape
    local_domains = basis_hbm.shape[0]
    rounds = points // SEND_POINTS
    parts = points // PART_POINTS
    per_part = PART_POINTS // SEND_POINTS
    moves = 2 * REACH
    band = lax.axis_index("band")
    grid = lax.axis_index("grid")
    me = band * grid_count + grid
    device_count = band_count * grid_count
    has_next = me + 1 < device_count
    has_prev = me > 0
    following = (me + 1) % device_count
    preceding = (me + device_count - 1) % device_count
    next_id = (following // grid_count, following % grid_count)
    prev_id = (preceding // grid_count, preceding % grid_count)

    def move_of(slot):
        return slot - REACH + slot // REACH

    def in_range(at_band):
        return (at_band >= 0) & (at_band < band_count)

    def wrapped(at_band):
        return (at_band + band_count) % band_count

    x_copy = pltpu.make_async_copy(x_hbm, x, local_sem.at[0])
    x_copy.start()
    basis_copies = []
    for d in range(local_domains):
        for k in range(rows):
            basis_copies.append(
                pltpu.make_async_copy(
                    basis_hbm.at[d, :, pl.ds(k * width, width)],
                    basis.at[d * rows + k],
                    basis_sem.at[d * rows + k],
                )
            )
    for copy in basis_copies:
        copy.start()
    pot_in[...] = jnp.zeros_like(pot_in)
    basis[local_domains * rows] = jnp.zeros((points, width), BF16)

    barrier = pltpu.get_barrier_semaphore()
    partners = [(has_next, next_id), (has_prev, prev_id)]
    for slot in range(moves):
        other = band + move_of(slot)
        partners.append((in_range(other), (wrapped(other), grid)))
    for live, target in partners:

        @pl.when(live)
        def _(target=target):
            pl.semaphore_signal(barrier, inc=1, device_id=target, device_id_type=MESH)

    def up_copies(step):
        return [
            pltpu.make_async_remote_copy(
                src_ref=narrow.at[step, rows - 2, pl.ds(2, 1)],
                dst_ref=above.at[step, pl.ds(0, 1)],
                send_sem=halo_send.at[step, 0],
                recv_sem=halo_recv.at[step, 0],
                device_id=next_id,
                device_id_type=MESH,
            ),
            pltpu.make_async_remote_copy(
                src_ref=narrow.at[step, rows - 1, pl.ds(1, 2)],
                dst_ref=above.at[step, pl.ds(1, 2)],
                send_sem=halo_send.at[step, 1],
                recv_sem=halo_recv.at[step, 1],
                device_id=next_id,
                device_id_type=MESH,
            ),
        ]

    def down_copies(step):
        return [
            pltpu.make_async_remote_copy(
                src_ref=narrow.at[step, 0, pl.ds(0, 2)],
                dst_ref=below.at[step, pl.ds(0, 2)],
                send_sem=halo_send.at[step, 2],
                recv_sem=halo_recv.at[step, 2],
                device_id=prev_id,
                device_id_type=MESH,
            ),
            pltpu.make_async_remote_copy(
                src_ref=narrow.at[step, 1, pl.ds(0, 1)],
                dst_ref=below.at[step, pl.ds(2, 1)],
                send_sem=halo_send.at[step, 3],
                recv_sem=halo_recv.at[step, 3],
                device_id=prev_id,
                device_id_type=MESH,
            ),
        ]

    up_set = [(rows - 2, 2), (rows - 1, 1), (rows - 1, 2)]
    down_set = [(0, 0), (0, 1), (1, 0)]
    inner_set = [
        (row, q)
        for row in range(rows)
        for q in range(3)
        if (row, q) not in up_set and (row, q) not in down_set
    ]

    def start_up(step):
        @pl.when(has_next)
        def _():
            for copy in up_copies(step):
                copy.start()

    def start_down(step):
        @pl.when(has_prev)
        def _():
            for copy in down_copies(step):
                copy.start()

    def basis_copy_of(slot, part):
        window = pl.ds(part * SEND_POINTS, SEND_POINTS)
        return pltpu.make_async_remote_copy(
            src_ref=packed.at[slot, window],
            dst_ref=arrived.at[slot, window],
            send_sem=basis_send.at[slot, part],
            recv_sem=basis_recv.at[slot, part],
            device_id=(wrapped(band + move_of(slot)), grid),
            device_id_type=MESH,
        )

    halves = band_count // 2
    parity = band % 2
    partner = wrapped(band + 1 - 2 * parity)
    has_partner = in_range(band + 1 - 2 * parity)
    level = band // 2
    rising = rounds * (halves - 1 - level) // halves
    falling = rounds * level // halves
    hops = jnp.where(has_partner, jnp.where(parity == 1, rising, falling), 0)
    passing = jnp.where(has_partner, jnp.where(parity == 1, falling, rising), 0)

    def hop_copy(slot, part):
        window = pl.ds(part * SEND_POINTS, SEND_POINTS)
        return pltpu.make_async_remote_copy(
            src_ref=packed.at[slot, window],
            dst_ref=transit.at[window],
            send_sem=basis_send.at[slot, part],
            recv_sem=hop_recv.at[part],
            device_id=(partner, grid),
            device_id_type=MESH,
        )

    def forward_copy(slot, part):
        window = pl.ds(part * SEND_POINTS, SEND_POINTS)
        return pltpu.make_async_remote_copy(
            src_ref=transit.at[window],
            dst_ref=arrived.at[slot, window],
            send_sem=hop_send.at[part],
            recv_sem=basis_recv.at[slot, part],
            device_id=(wrapped(band + 2 * move_of(slot)), grid),
            device_id_type=MESH,
        )

    def start_hop(part, carry):
        for slot in (1, 2):

            @pl.when((parity == slot - 1) & (part < hops))
            def _(slot=slot):
                hop_copy(slot, part).start()

        return carry

    def forward(part):
        for slot in (1, 2):

            @pl.when((parity == 2 - slot) & (part < passing))
            def _(slot=slot):
                hop_copy(slot, part).wait_recv()
                forward_copy(slot, part).start()

    def forward_part(part, carry):
        forward(part)
        return carry

    def start_round(part):
        for slot in (1, 2, 0, 3):
            direct = in_range(band + move_of(slot))
            if slot in (1, 2):
                direct = direct & jnp.logical_not((parity == slot - 1) & (part < hops))

            @pl.when(direct)
            def _(slot=slot):
                basis_copy_of(slot, part).start()

    x_copy.wait()
    for row, q in up_set:
        narrow[0, row, q] = x[row, q].astype(BF16)
    for row, q in down_set:
        narrow[0, row, q] = x[row, q].astype(BF16)
    for row, q in inner_set:
        narrow[0, row, q] = x[row, q].astype(BF16)

    @pl.when(jnp.logical_not(has_next))
    def _():
        below[...] = jnp.zeros_like(below)

    @pl.when(jnp.logical_not(has_prev))
    def _():
        above[...] = jnp.zeros_like(above)

    for copy in basis_copies:
        copy.wait()
    firsts = []
    counts = []
    own_moves = []
    for d in range(local_domains):
        row_at = me * local_domains + d
        first = blocks_ref[0, row_at]
        firsts.append(first)
        live = jnp.int32(0)
        for k in range(blocks_ref.shape[0]):
            live = live + (blocks_ref[k, row_at] >= 0).astype(jnp.int32)
        counts.append(live)
        own_moves.append(lax.div(lax.div(first, jnp.int32(rows)), jnp.int32(grid_count)) - band)
    plans = []
    for slot in range(moves + 1):
        move = 0 if slot == moves else slot - REACH + slot // REACH
        chosen = jnp.int32(local_domains)
        offset = jnp.int32(0)
        count = jnp.int32(0)
        for d in range(local_domains):
            hit = own_moves[d] == move
            chosen = jnp.where(hit, d, chosen)
            offset = jnp.where(hit, lax.rem(firsts[d], jnp.int32(rows)), offset)
            count = jnp.where(hit, counts[d], count)
        places = []
        for k in range(rows):
            live = (k >= offset) & (k < offset + count)
            places.append(jnp.where(live, chosen * rows + k - offset, local_domains * rows))
        plans.append(places)

    def pack_part(part):
        window = pl.ds(pl.multiple_of(part * SEND_POINTS, SEND_POINTS), SEND_POINTS)
        for slot, places in enumerate(plans):
            for k, place in enumerate(places):
                value = basis[place, window]
                if slot == moves:
                    arrived[moves, window, k * width : (k + 1) * width] = value
                else:
                    packed[slot, window, k * width : (k + 1) * width] = value

    def pack_one(part, carry):
        pack_part(part)
        return carry

    lax.fori_loop(0, rounds, pack_one, 0)

    peers = jnp.int32(0)
    for live, _ in partners:
        peers = peers + live.astype(jnp.int32)
    pl.semaphore_wait(barrier, peers)
    start_up(0)
    start_down(0)

    at_edge = (grid == 0) | (grid == grid_count - 1)

    def start_part(part, carry):
        start_round(part)
        return carry

    def start_all():
        lax.fori_loop(0, rounds, start_hop, 0)
        lax.fori_loop(0, rounds, start_part, 0)

    @pl.when(jnp.logical_not(at_edge))
    def _():
        start_all()

    def block_at(step, row, q):
        if 0 <= row < rows:
            return narrow[step, row, q]
        if row < 0:
            return above[step, {(-2, 2): 0, (-1, 1): 1, (-1, 2): 2}[(row, q)]]
        return below[step, {(0, 0): 0, (0, 1): 1, (1, 0): 2}[(row - rows, q)]]

    def update(step, row, q):
        gap = 2 - q
        column = row - gap
        total = None
        for middle in range(row - 2, column + 3):
            left_turned = middle > row
            left = block_at(step, max(row, middle), 2 - abs(row - middle))
            right_turned = middle < column
            right = block_at(step, max(column, middle), 2 - abs(column - middle))
            term = product(left, right, left_turned, right_turned)
            total = term if total is None else total + term
        chosen = jnp.broadcast_to(choices_ref[step], total.shape) == 1
        fresh = jnp.where(chosen, 2.0 * x[row, q] - total, total)
        x[row, q] = fresh
        narrow[step + 1, row, q] = fresh.astype(BF16)

    def purify(step, carry):
        @pl.when(has_next)
        def _():
            for copy in down_copies(step):
                copy.wait_recv()

        for row, q in up_set:
            update(step, row, q)

        @pl.when(step + 1 < ITERS)
        def _():
            start_up(step + 1)

        @pl.when(has_prev)
        def _():
            for copy in up_copies(step):
                copy.wait_recv()

        for row, q in down_set:
            update(step, row, q)

        @pl.when(step + 1 < ITERS)
        def _():
            start_down(step + 1)

        @pl.when(at_edge & (step == EDGE_STEP))
        def _():
            start_all()

        @pl.when(jnp.logical_not(at_edge) & (step > 0))
        def _():
            lax.fori_loop((step - 1) * STEP_HOPS, step * STEP_HOPS, forward_part, 0)

        for row, q in inner_set:
            update(step, row, q)
        return carry

    lax.fori_loop(0, ITERS, purify, 0)
    for k in range(rows):
        for gap in range(3):
            if k + gap < rows:
                tile = narrow[ITERS, k + gap, 2 - gap]
                tiles[k, gap * width : (gap + 1) * width] = tile if gap == 0 else tile * jnp.asarray(2.0, BF16)
    ham[...] = jnp.zeros_like(ham)
    factor = (rows * width) / points

    def domain_part(slot, part):
        window = pl.ds(pl.multiple_of(part * PART_POINTS, PART_POINTS), PART_POINTS)

        def phi(first, last):
            return arrived[slot, window, first * width : last * width]

        summed = None
        for k in range(rows):
            last = min(k + 3, rows)
            applied = product(phi(k, last), tiles[k, : (last - k) * width], False, False)
            term = applied * phi(k, k + 1).astype(F32)
            summed = term if summed is None else summed + term
        potential = jnp.tanh(jnp.sum(summed, axis=1, keepdims=True))
        scale = factor * potential
        for k in range(rows):
            psi[:, k * width : (k + 1) * width] = (scale * phi(k, k + 1).astype(F32)).astype(BF16)
        for k in range(rows):
            first = max(k - 2, 0)
            found = product(psi[:, k * width : (k + 1) * width], phi(first, k + 1), True, False)
            for at in range(first, k + 1):
                ham[k, 2 - k + at] += found[:, (at - first) * width : (at - first + 1) * width]
        return jnp.transpose(jnp.broadcast_to(potential, (PART_POINTS, 128)))[:8]

    def own_part(part, carry):
        pot_in[moves, part] = domain_part(moves, part)
        return carry

    lax.fori_loop(0, parts, own_part, 0)

    def pot_copy(slot, part):
        return pltpu.make_async_remote_copy(
            src_ref=pot_out.at[slot, part],
            dst_ref=pot_in.at[slot, part],
            send_sem=pot_send.at[slot, part],
            recv_sem=pot_recv.at[slot, part],
            device_id=(wrapped(band - move_of(slot)), grid),
            device_id_type=MESH,
        )

    forwarded = jnp.where(at_edge, 0, (ITERS - 1) * STEP_HOPS)

    def other_part(index, carry):
        @pl.when(forwarded + index < rounds)
        def _():
            forward(forwarded + index)

        part = index // moves
        slot = (index % moves) * (moves - 1) % moves

        @pl.when(in_range(band - move_of(slot)))
        def _():
            for piece in range(per_part):
                basis_copy_of(slot, part * per_part + piece).wait_recv()
            pot_out[slot, part] = domain_part(slot, part)
            pot_copy(slot, part).start()

        return carry

    lax.fori_loop(0, parts * moves, other_part, 0)

    def settle_halo(step, carry):
        @pl.when(has_next)
        def _():
            for copy in up_copies(step):
                copy.wait_send()

        @pl.when(has_prev)
        def _():
            for copy in down_copies(step):
                copy.wait_send()

        return carry

    lax.fori_loop(0, ITERS, settle_halo, 0)

    def settle_basis(index, carry):
        slot = index // rounds

        @pl.when(in_range(band + move_of(slot)))
        def _():
            basis_copy_of(slot, index % rounds).wait_send()

        return carry

    lax.fori_loop(0, moves * rounds, settle_basis, 0)

    def settle_hop(part, carry):
        for slot in (1, 2):

            @pl.when((parity == 2 - slot) & (part < passing))
            def _(slot=slot):
                forward_copy(slot, part).wait_send()

        return carry

    lax.fori_loop(0, rounds, settle_hop, 0)

    def settle_pot(index, carry):
        slot = index // parts
        part = index % parts

        @pl.when(in_range(band - move_of(slot)))
        def _():
            pot_copy(slot, part).wait_send()

        @pl.when(in_range(band + move_of(slot)))
        def _():
            pot_copy(slot, part).wait_recv()

        return carry

    lax.fori_loop(0, moves * parts, settle_pot, 0)
    for d in range(local_domains):
        chosen = jnp.int32(moves)
        for slot in range(moves):
            chosen = jnp.where(own_moves[d] == move_of(slot), slot, chosen)
        for part in range(parts):
            window = slice(part * PART_POINTS, (part + 1) * PART_POINTS)
            potential_ref[d : d + 1, window] = pot_in[chosen, part][:1]


def solution(mesh):
    band_count = mesh.shape["band"]
    grid_count = mesh.shape["grid"]

    def body(x_initial, sp2_choices, domain_blocks, basis_values):
        rows, gaps, width, _ = x_initial.shape
        local_domains, points, columns = basis_values.shape
        moves = 2 * REACH
        rounds = points // SEND_POINTS
        parts = points // PART_POINTS
        smem = pl.BlockSpec(memory_space=pltpu.SMEM)
        anywhere = pl.BlockSpec(memory_space=pl.ANY)
        in_vmem = pl.BlockSpec(memory_space=pltpu.VMEM)
        return pl.pallas_call(
            functools.partial(kernel, band_count, grid_count),
            out_shape=(
                jax.ShapeDtypeStruct(x_initial.shape, F32),
                jax.ShapeDtypeStruct(x_initial.shape, F32),
                jax.ShapeDtypeStruct((local_domains, points), F32),
            ),
            in_specs=[smem, smem, anywhere, anywhere],
            out_specs=(in_vmem, in_vmem, in_vmem),
            scratch_shapes=[
                pltpu.VMEM((local_domains * rows + 1, points, width), BF16),
                pltpu.VMEM((ITERS + 1,) + x_initial.shape, BF16),
                pltpu.VMEM((rows, 3 * width, width), BF16),
                pltpu.VMEM((ITERS, 3, width, width), BF16),
                pltpu.VMEM((ITERS, 3, width, width), BF16),
                pltpu.VMEM((moves, points, columns), BF16),
                pltpu.VMEM((moves + 1, points, columns), BF16),
                pltpu.VMEM((points, columns), BF16),
                pltpu.VMEM((PART_POINTS, columns), BF16),
                pltpu.VMEM((moves + 1, parts, 8, PART_POINTS), F32),
                pltpu.VMEM((moves, parts, 8, PART_POINTS), F32),
                pltpu.SemaphoreType.DMA((1,)),
                pltpu.SemaphoreType.DMA((local_domains * rows,)),
                pltpu.SemaphoreType.DMA((ITERS, 4)),
                pltpu.SemaphoreType.DMA((ITERS, 4)),
                pltpu.SemaphoreType.DMA((moves, rounds)),
                pltpu.SemaphoreType.DMA((moves, rounds)),
                pltpu.SemaphoreType.DMA((rounds,)),
                pltpu.SemaphoreType.DMA((rounds,)),
                pltpu.SemaphoreType.DMA((moves, parts)),
                pltpu.SemaphoreType.DMA((moves, parts)),
            ],
            compiler_params=pltpu.CompilerParams(
                collective_id=0, has_side_effects=True, vmem_limit_bytes=VMEM_LIMIT
            ),
        )(domain_blocks.T, sp2_choices, x_initial, basis_values)

    placed = (P(("band", "grid"), None, None, None), P(), P(), P(("band", "grid"), None, None))
    return jax.shard_map(
        body,
        mesh=mesh,
        in_specs=placed,
        out_specs=(
            P(("band", "grid"), None, None, None),
            P(("band", "grid"), None, None, None),
            P(("band", "grid"), None),
        ),
        check_vma=False,
    )
```

```python
import functools

import jax
import jax.numpy as jnp
from jax import lax
from jax.experimental import pallas as pl
from jax.experimental.pallas import tpu as pltpu
from jax.sharding import PartitionSpec as P

REACH = 2
ITERS = 4
SEND_POINTS = 64
PART_POINTS = 256
EDGE_STEP = ITERS - 2
STEP_HOPS = 4
VMEM_LIMIT = 48000000
SMALL_LIMIT = 1000000
MESH = pl.DeviceIdType.MESH
F32 = jnp.float32
BF16 = jnp.bfloat16


def product(left, right, left_turned, right_turned):
    dims = (((0 if left_turned else 1,), (1 if right_turned else 0,)), ((), ()))
    return lax.dot_general(left, right, dims, preferred_element_type=F32)


def kernel(
    band_count,
    grid_count,
    blocks_hbm,
    choices_hbm,
    x_hbm,
    basis_hbm,
    x,
    ham,
    potential_ref,
    basis,
    narrow,
    tiles,
    above,
    below,
    packed,
    arrived,
    transit,
    psi,
    pot_in,
    pot_out,
    blocks_ref,
    choices_ref,
    local_sem,
    basis_sem,
    halo_send,
    halo_recv,
    basis_send,
    basis_recv,
    hop_send,
    hop_recv,
    pot_send,
    pot_recv,
):
    rows, _, width, _ = x.shape
    _, points, _ = basis_hbm.shape
    local_domains = basis_hbm.shape[0]
    rounds = points // SEND_POINTS
    parts = points // PART_POINTS
    per_part = PART_POINTS // SEND_POINTS
    moves = 2 * REACH
    band = lax.axis_index("band")
    grid = lax.axis_index("grid")
    me = band * grid_count + grid
    device_count = band_count * grid_count
    has_next = me + 1 < device_count
    has_prev = me > 0
    following = (me + 1) % device_count
    preceding = (me + device_count - 1) % device_count
    next_id = (following // grid_count, following % grid_count)
    prev_id = (preceding // grid_count, preceding % grid_count)

    def move_of(slot):
        return slot - REACH + slot // REACH

    def in_range(at_band):
        return (at_band >= 0) & (at_band < band_count)

    def wrapped(at_band):
        return (at_band + band_count) % band_count

    blocks_copy = pltpu.make_async_copy(blocks_hbm, blocks_ref, local_sem.at[1])
    blocks_copy.start()
    choices_copy = pltpu.make_async_copy(choices_hbm, choices_ref, local_sem.at[2])
    choices_copy.start()
    x_copy = pltpu.make_async_copy(x_hbm, x, local_sem.at[0])
    x_copy.start()
    basis_copies = []
    for d in range(local_domains):
        for k in range(rows):
            basis_copies.append(
                pltpu.make_async_copy(
                    basis_hbm.at[d, :, pl.ds(k * width, width)],
                    basis.at[d * rows + k],
                    basis_sem.at[d * rows + k],
                )
            )
    for copy in basis_copies:
        copy.start()
    pot_in[...] = jnp.zeros_like(pot_in)
    basis[local_domains * rows] = jnp.zeros((points, width), BF16)

    barrier = pltpu.get_barrier_semaphore()
    partners = [(has_next, next_id), (has_prev, prev_id)]
    for slot in range(moves):
        other = band + move_of(slot)
        partners.append((in_range(other), (wrapped(other), grid)))
    for live, target in partners:

        @pl.when(live)
        def _(target=target):
            pl.semaphore_signal(barrier, inc=1, device_id=target, device_id_type=MESH)

    def up_copies(step):
        return [
            pltpu.make_async_remote_copy(
                src_ref=narrow.at[step, rows - 2, pl.ds(2, 1)],
                dst_ref=above.at[step, pl.ds(0, 1)],
                send_sem=halo_send.at[step, 0],
                recv_sem=halo_recv.at[step, 0],
                device_id=next_id,
                device_id_type=MESH,
            ),
            pltpu.make_async_remote_copy(
                src_ref=narrow.at[step, rows - 1, pl.ds(1, 2)],
                dst_ref=above.at[step, pl.ds(1, 2)],
                send_sem=halo_send.at[step, 1],
                recv_sem=halo_recv.at[step, 1],
                device_id=next_id,
                device_id_type=MESH,
            ),
        ]

    def down_copies(step):
        return [
            pltpu.make_async_remote_copy(
                src_ref=narrow.at[step, 0, pl.ds(0, 2)],
                dst_ref=below.at[step, pl.ds(0, 2)],
                send_sem=halo_send.at[step, 2],
                recv_sem=halo_recv.at[step, 2],
                device_id=prev_id,
                device_id_type=MESH,
            ),
            pltpu.make_async_remote_copy(
                src_ref=narrow.at[step, 1, pl.ds(0, 1)],
                dst_ref=below.at[step, pl.ds(2, 1)],
                send_sem=halo_send.at[step, 3],
                recv_sem=halo_recv.at[step, 3],
                device_id=prev_id,
                device_id_type=MESH,
            ),
        ]

    up_set = [(rows - 2, 2), (rows - 1, 1), (rows - 1, 2)]
    down_set = [(0, 0), (0, 1), (1, 0)]
    inner_set = [
        (row, q)
        for row in range(rows)
        for q in range(3)
        if (row, q) not in up_set and (row, q) not in down_set
    ]

    def start_up(step):
        @pl.when(has_next)
        def _():
            for copy in up_copies(step):
                copy.start()

    def start_down(step):
        @pl.when(has_prev)
        def _():
            for copy in down_copies(step):
                copy.start()

    def basis_copy_of(slot, part):
        window = pl.ds(part * SEND_POINTS, SEND_POINTS)
        return pltpu.make_async_remote_copy(
            src_ref=packed.at[slot, window],
            dst_ref=arrived.at[slot, window],
            send_sem=basis_send.at[slot, part],
            recv_sem=basis_recv.at[slot, part],
            device_id=(wrapped(band + move_of(slot)), grid),
            device_id_type=MESH,
        )

    halves = band_count // 2
    parity = band % 2
    partner = wrapped(band + 1 - 2 * parity)
    has_partner = in_range(band + 1 - 2 * parity)
    level = band // 2
    rising = rounds * (halves - 1 - level) // halves
    falling = rounds * level // halves
    hops = jnp.where(has_partner, jnp.where(parity == 1, rising, falling), 0)
    passing = jnp.where(has_partner, jnp.where(parity == 1, falling, rising), 0)

    def hop_copy(slot, part):
        window = pl.ds(part * SEND_POINTS, SEND_POINTS)
        return pltpu.make_async_remote_copy(
            src_ref=packed.at[slot, window],
            dst_ref=transit.at[window],
            send_sem=basis_send.at[slot, part],
            recv_sem=hop_recv.at[part],
            device_id=(partner, grid),
            device_id_type=MESH,
        )

    def forward_copy(slot, part):
        window = pl.ds(part * SEND_POINTS, SEND_POINTS)
        return pltpu.make_async_remote_copy(
            src_ref=transit.at[window],
            dst_ref=arrived.at[slot, window],
            send_sem=hop_send.at[part],
            recv_sem=basis_recv.at[slot, part],
            device_id=(wrapped(band + 2 * move_of(slot)), grid),
            device_id_type=MESH,
        )

    def start_hop(part, carry):
        for slot in (1, 2):

            @pl.when((parity == slot - 1) & (part < hops))
            def _(slot=slot):
                hop_copy(slot, part).start()

        return carry

    def forward(part):
        for slot in (1, 2):

            @pl.when((parity == 2 - slot) & (part < passing))
            def _(slot=slot):
                hop_copy(slot, part).wait_recv()
                forward_copy(slot, part).start()

    def forward_part(part, carry):
        forward(part)
        return carry

    def start_round(part):
        for slot in (0, 3, 1, 2):
            direct = in_range(band + move_of(slot))
            if slot in (1, 2):
                direct = direct & jnp.logical_not((parity == slot - 1) & (part < hops))

            @pl.when(direct)
            def _(slot=slot):
                basis_copy_of(slot, part).start()

    x_copy.wait()
    for row, q in up_set:
        narrow[0, row, q] = x[row, q].astype(BF16)
    for row, q in down_set:
        narrow[0, row, q] = x[row, q].astype(BF16)
    for row, q in inner_set:
        narrow[0, row, q] = x[row, q].astype(BF16)

    @pl.when(jnp.logical_not(has_next))
    def _():
        below[...] = jnp.zeros_like(below)

    @pl.when(jnp.logical_not(has_prev))
    def _():
        above[...] = jnp.zeros_like(above)

    for copy in basis_copies:
        copy.wait()
    blocks_copy.wait()
    choices_copy.wait()
    firsts = []
    counts = []
    own_moves = []
    for d in range(local_domains):
        row_at = me * local_domains + d
        first = blocks_ref[0, row_at]
        firsts.append(first)
        live = jnp.int32(0)
        for k in range(blocks_ref.shape[0]):
            live = live + (blocks_ref[k, row_at] >= 0).astype(jnp.int32)
        counts.append(live)
        own_moves.append(lax.div(lax.div(first, jnp.int32(rows)), jnp.int32(grid_count)) - band)
    plans = []
    for slot in range(moves + 1):
        move = 0 if slot == moves else slot - REACH + slot // REACH
        chosen = jnp.int32(local_domains)
        offset = jnp.int32(0)
        count = jnp.int32(0)
        for d in range(local_domains):
            hit = own_moves[d] == move
            chosen = jnp.where(hit, d, chosen)
            offset = jnp.where(hit, lax.rem(firsts[d], jnp.int32(rows)), offset)
            count = jnp.where(hit, counts[d], count)
        places = []
        for k in range(rows):
            live = (k >= offset) & (k < offset + count)
            places.append(jnp.where(live, chosen * rows + k - offset, local_domains * rows))
        plans.append(places)

    def pack_part(part):
        window = pl.ds(pl.multiple_of(part * SEND_POINTS, SEND_POINTS), SEND_POINTS)
        for slot, places in enumerate(plans):
            for k, place in enumerate(places):
                value = basis[place, window]
                if slot == moves:
                    arrived[moves, window, k * width : (k + 1) * width] = value
                else:
                    packed[slot, window, k * width : (k + 1) * width] = value

    def pack_one(part, carry):
        pack_part(part)
        return carry

    lax.fori_loop(0, rounds, pack_one, 0)

    peers = jnp.int32(0)
    for live, _ in partners:
        peers = peers + live.astype(jnp.int32)
    pl.semaphore_wait(barrier, peers)
    start_up(0)
    start_down(0)

    at_edge = (grid == 0) | (grid == grid_count - 1)

    def start_part(part, carry):
        start_round(part)
        return carry

    def start_all():
        lax.fori_loop(0, rounds, start_hop, 0)
        lax.fori_loop(0, rounds, start_part, 0)

    @pl.when(jnp.logical_not(at_edge))
    def _():
        start_all()

    def block_at(step, row, q):
        if 0 <= row < rows:
            return narrow[step, row, q]
        if row < 0:
            return above[step, {(-2, 2): 0, (-1, 1): 1, (-1, 2): 2}[(row, q)]]
        return below[step, {(0, 0): 0, (0, 1): 1, (1, 0): 2}[(row - rows, q)]]

    def update(step, row, q):
        gap = 2 - q
        column = row - gap
        total = None
        for middle in range(row - 2, column + 3):
            left_turned = middle > row
            left = block_at(step, max(row, middle), 2 - abs(row - middle))
            right_turned = middle < column
            right = block_at(step, max(column, middle), 2 - abs(column - middle))
            term = product(left, right, left_turned, right_turned)
            total = term if total is None else total + term
        chosen = jnp.broadcast_to(choices_ref[step], total.shape) == 1
        fresh = jnp.where(chosen, 2.0 * x[row, q] - total, total)
        x[row, q] = fresh
        narrow[step + 1, row, q] = fresh.astype(BF16)

    def purify(step, carry):
        @pl.when(has_next)
        def _():
            for copy in down_copies(step):
                copy.wait_recv()

        for row, q in up_set:
            update(step, row, q)

        @pl.when(step + 1 < ITERS)
        def _():
            start_up(step + 1)

        @pl.when(has_prev)
        def _():
            for copy in up_copies(step):
                copy.wait_recv()

        for row, q in down_set:
            update(step, row, q)

        @pl.when(step + 1 < ITERS)
        def _():
            start_down(step + 1)

        @pl.when(at_edge & (step == EDGE_STEP))
        def _():
            start_all()

        @pl.when(jnp.logical_not(at_edge) & (step > 0))
        def _():
            lax.fori_loop((step - 1) * STEP_HOPS, step * STEP_HOPS, forward_part, 0)

        for row, q in inner_set:
            update(step, row, q)
        return carry

    lax.fori_loop(0, ITERS, purify, 0)
    for k in range(rows):
        for gap in range(3):
            if k + gap < rows:
                tile = narrow[ITERS, k + gap, 2 - gap]
                tiles[k, gap * width : (gap + 1) * width] = tile if gap == 0 else tile * jnp.asarray(2.0, BF16)
    ham[...] = jnp.zeros_like(ham)
    factor = (rows * width) / points

    def domain_part(slot, part, publish):
        window = pl.ds(pl.multiple_of(part * PART_POINTS, PART_POINTS), PART_POINTS)

        def phi(first, last):
            return arrived[slot, window, first * width : last * width]

        summed = None
        for k in range(rows):
            last = min(k + 3, rows)
            applied = product(phi(k, last), tiles[k, : (last - k) * width], False, False)
            term = applied * phi(k, k + 1).astype(F32)
            summed = term if summed is None else summed + term
        potential = jnp.tanh(jnp.sum(summed, axis=1, keepdims=True))
        publish(jnp.transpose(jnp.broadcast_to(potential, (PART_POINTS, 128)))[:8])
        scale = factor * potential
        for k in range(rows):
            psi[:, k * width : (k + 1) * width] = (scale * phi(k, k + 1).astype(F32)).astype(BF16)
        for k in range(rows):
            first = max(k - 2, 0)
            found = product(psi[:, k * width : (k + 1) * width], phi(first, k + 1), True, False)
            for at in range(first, k + 1):
                ham[k, 2 - k + at] += found[:, (at - first) * width : (at - first + 1) * width]

    def own_part(part, carry):
        def publish(value):
            pot_in[moves, part] = value

        domain_part(moves, part, publish)
        return carry

    lax.fori_loop(0, parts, own_part, 0)

    def pot_copy(slot, part):
        return pltpu.make_async_remote_copy(
            src_ref=pot_out.at[slot, part],
            dst_ref=pot_in.at[slot, part],
            send_sem=pot_send.at[slot, part],
            recv_sem=pot_recv.at[slot, part],
            device_id=(wrapped(band - move_of(slot)), grid),
            device_id_type=MESH,
        )

    forwarded = jnp.where(at_edge, 0, (ITERS - 1) * STEP_HOPS)

    def other_part(index, carry):
        reached = jnp.minimum(forwarded + index * STEP_HOPS, rounds)
        lax.fori_loop(reached, jnp.minimum(reached + STEP_HOPS, rounds), forward_part, 0)

        part = index // moves
        slot = (index % moves) * (moves - 1) % moves

        @pl.when(in_range(band - move_of(slot)))
        def _():
            for piece in range(per_part):
                basis_copy_of(slot, part * per_part + piece).wait_recv()

            def publish(value):
                pot_out[slot, part] = value
                pot_copy(slot, part).start()

            domain_part(slot, part, publish)

        return carry

    lax.fori_loop(0, parts * moves, other_part, 0)

    def settle_halo(step, carry):
        @pl.when(has_next)
        def _():
            for copy in up_copies(step):
                copy.wait_send()

        @pl.when(has_prev)
        def _():
            for copy in down_copies(step):
                copy.wait_send()

        return carry

    lax.fori_loop(0, ITERS, settle_halo, 0)

    def settle_basis(index, carry):
        slot = index // rounds

        @pl.when(in_range(band + move_of(slot)))
        def _():
            basis_copy_of(slot, index % rounds).wait_send()

        return carry

    lax.fori_loop(0, moves * rounds, settle_basis, 0)

    def settle_hop(part, carry):
        for slot in (1, 2):

            @pl.when((parity == 2 - slot) & (part < passing))
            def _(slot=slot):
                forward_copy(slot, part).wait_send()

        return carry

    lax.fori_loop(0, rounds, settle_hop, 0)

    def settle_pot(index, carry):
        slot = index // parts
        part = index % parts

        @pl.when(in_range(band - move_of(slot)))
        def _():
            pot_copy(slot, part).wait_send()

        @pl.when(in_range(band + move_of(slot)))
        def _():
            pot_copy(slot, part).wait_recv()

        return carry

    lax.fori_loop(0, moves * parts, settle_pot, 0)
    for d in range(local_domains):
        chosen = jnp.int32(moves)
        for slot in range(moves):
            chosen = jnp.where(own_moves[d] == move_of(slot), slot, chosen)
        for part in range(parts):
            window = slice(part * PART_POINTS, (part + 1) * PART_POINTS)
            potential_ref[d : d + 1, window] = pot_in[chosen, part][:1]


def write_out(*refs):
    count = len(refs) // 2
    sem = refs[-1]
    copies = [pltpu.make_async_copy(refs[at], refs[count + at], sem.at[at]) for at in range(count)]
    for copy in copies:
        copy.start()
    for copy in copies:
        copy.wait()


def solution(mesh):
    band_count = mesh.shape["band"]
    grid_count = mesh.shape["grid"]

    def body(x_initial, sp2_choices, domain_blocks, basis_values):
        rows, gaps, width, _ = x_initial.shape
        local_domains, points, columns = basis_values.shape
        moves = 2 * REACH
        rounds = points // SEND_POINTS
        parts = points // PART_POINTS
        in_hbm = pl.BlockSpec(memory_space=pltpu.HBM)
        anywhere = pl.BlockSpec(memory_space=pl.ANY)
        in_vmem = pl.BlockSpec(memory_space=pltpu.VMEM)
        results = pl.pallas_call(
            functools.partial(kernel, band_count, grid_count),
            out_shape=(
                jax.ShapeDtypeStruct(x_initial.shape, F32),
                jax.ShapeDtypeStruct(x_initial.shape, F32),
                jax.ShapeDtypeStruct((local_domains, points), F32),
            ),
            in_specs=[in_hbm, in_hbm, anywhere, anywhere],
            out_specs=(in_vmem, in_vmem, in_vmem),
            scratch_shapes=[
                pltpu.VMEM((local_domains * rows + 1, points, width), BF16),
                pltpu.VMEM((ITERS + 1,) + x_initial.shape, BF16),
                pltpu.VMEM((rows, 3 * width, width), BF16),
                pltpu.VMEM((ITERS, 3, width, width), BF16),
                pltpu.VMEM((ITERS, 3, width, width), BF16),
                pltpu.VMEM((moves, points, columns), BF16),
                pltpu.VMEM((moves + 1, points, columns), BF16),
                pltpu.VMEM((points, columns), BF16),
                pltpu.VMEM((PART_POINTS, columns), BF16),
                pltpu.VMEM((moves + 1, parts, 8, PART_POINTS), F32),
                pltpu.VMEM((moves, parts, 8, PART_POINTS), F32),
                pltpu.SMEM(domain_blocks.shape[::-1], jnp.int32),
                pltpu.SMEM(sp2_choices.shape, jnp.int32),
                pltpu.SemaphoreType.DMA((3,)),
                pltpu.SemaphoreType.DMA((local_domains * rows,)),
                pltpu.SemaphoreType.DMA((ITERS, 4)),
                pltpu.SemaphoreType.DMA((ITERS, 4)),
                pltpu.SemaphoreType.DMA((moves, rounds)),
                pltpu.SemaphoreType.DMA((moves, rounds)),
                pltpu.SemaphoreType.DMA((rounds,)),
                pltpu.SemaphoreType.DMA((rounds,)),
                pltpu.SemaphoreType.DMA((moves, parts)),
                pltpu.SemaphoreType.DMA((moves, parts)),
            ],
            compiler_params=pltpu.CompilerParams(
                collective_id=0, has_side_effects=True, vmem_limit_bytes=VMEM_LIMIT
            ),
        )(domain_blocks.T, sp2_choices, x_initial, basis_values)
        return pl.pallas_call(
            write_out,
            out_shape=tuple(jax.ShapeDtypeStruct(held.shape, held.dtype) for held in results),
            in_specs=[in_vmem] * len(results),
            out_specs=(in_hbm,) * len(results),
            scratch_shapes=[pltpu.SemaphoreType.DMA((len(results),))],
            compiler_params=pltpu.CompilerParams(vmem_limit_bytes=SMALL_LIMIT),
        )(*results)

    placed = (P(("band", "grid"), None, None, None), P(), P(), P(("band", "grid"), None, None))
    return jax.shard_map(
        body,
        mesh=mesh,
        in_specs=placed,
        out_specs=(
            P(("band", "grid"), None, None, None),
            P(("band", "grid"), None, None, None),
            P(("band", "grid"), None),
        ),
        check_vma=False,
    )
```

```python
import functools

import jax
import jax.numpy as jnp
from jax import lax
from jax.experimental import pallas as pl
from jax.experimental.pallas import tpu as pltpu
from jax.sharding import PartitionSpec as P

REACH = 2
ITERS = 4
SEND_POINTS = 64
PART_POINTS = 256
EDGE_STEP = ITERS - 2
STEP_HOPS = 3
VMEM_LIMIT = 48000000
SMALL_LIMIT = 1000000
MESH = pl.DeviceIdType.MESH
F32 = jnp.float32
BF16 = jnp.bfloat16


def product(left, right, left_turned, right_turned):
    dims = (((0 if left_turned else 1,), (1 if right_turned else 0,)), ((), ()))
    return lax.dot_general(left, right, dims, preferred_element_type=F32)


def kernel(
    band_count,
    grid_count,
    blocks_hbm,
    choices_hbm,
    x_hbm,
    basis_hbm,
    x,
    ham,
    potential_ref,
    basis,
    narrow,
    tiles,
    above,
    below,
    packed,
    arrived,
    transit,
    psi,
    pot_in,
    pot_out,
    blocks_ref,
    choices_ref,
    local_sem,
    basis_sem,
    halo_send,
    halo_recv,
    basis_send,
    basis_recv,
    hop_send,
    hop_recv,
    pot_send,
    pot_recv,
):
    rows, _, width, _ = x.shape
    _, points, _ = basis_hbm.shape
    local_domains = basis_hbm.shape[0]
    rounds = points // SEND_POINTS
    parts = points // PART_POINTS
    per_part = PART_POINTS // SEND_POINTS
    moves = 2 * REACH
    band = lax.axis_index("band")
    grid = lax.axis_index("grid")
    me = band * grid_count + grid
    device_count = band_count * grid_count
    has_next = me + 1 < device_count
    has_prev = me > 0
    following = (me + 1) % device_count
    preceding = (me + device_count - 1) % device_count
    next_id = (following // grid_count, following % grid_count)
    prev_id = (preceding // grid_count, preceding % grid_count)

    def move_of(slot):
        return slot - REACH + slot // REACH

    def in_range(at_band):
        return (at_band >= 0) & (at_band < band_count)

    def wrapped(at_band):
        return (at_band + band_count) % band_count

    blocks_copy = pltpu.make_async_copy(blocks_hbm, blocks_ref, local_sem.at[1])
    blocks_copy.start()
    choices_copy = pltpu.make_async_copy(choices_hbm, choices_ref, local_sem.at[2])
    choices_copy.start()
    x_copy = pltpu.make_async_copy(x_hbm, x, local_sem.at[0])
    x_copy.start()
    basis_copies = []
    for d in range(local_domains):
        for k in range(rows):
            basis_copies.append(
                pltpu.make_async_copy(
                    basis_hbm.at[d, :, pl.ds(k * width, width)],
                    basis.at[d * rows + k],
                    basis_sem.at[d * rows + k],
                )
            )
    for copy in basis_copies:
        copy.start()
    pot_in[...] = jnp.zeros_like(pot_in)
    basis[local_domains * rows] = jnp.zeros((points, width), BF16)

    barrier = pltpu.get_barrier_semaphore()
    partners = [(has_next, next_id), (has_prev, prev_id)]
    for slot in range(moves):
        other = band + move_of(slot)
        partners.append((in_range(other), (wrapped(other), grid)))
    for live, target in partners:

        @pl.when(live)
        def _(target=target):
            pl.semaphore_signal(barrier, inc=1, device_id=target, device_id_type=MESH)

    def up_copies(step):
        return [
            pltpu.make_async_remote_copy(
                src_ref=narrow.at[step, rows - 2, pl.ds(2, 1)],
                dst_ref=above.at[step, pl.ds(0, 1)],
                send_sem=halo_send.at[step, 0],
                recv_sem=halo_recv.at[step, 0],
                device_id=next_id,
                device_id_type=MESH,
            ),
            pltpu.make_async_remote_copy(
                src_ref=narrow.at[step, rows - 1, pl.ds(1, 2)],
                dst_ref=above.at[step, pl.ds(1, 2)],
                send_sem=halo_send.at[step, 1],
                recv_sem=halo_recv.at[step, 1],
                device_id=next_id,
                device_id_type=MESH,
            ),
        ]

    def down_copies(step):
        return [
            pltpu.make_async_remote_copy(
                src_ref=narrow.at[step, 0, pl.ds(0, 2)],
                dst_ref=below.at[step, pl.ds(0, 2)],
                send_sem=halo_send.at[step, 2],
                recv_sem=halo_recv.at[step, 2],
                device_id=prev_id,
                device_id_type=MESH,
            ),
            pltpu.make_async_remote_copy(
                src_ref=narrow.at[step, 1, pl.ds(0, 1)],
                dst_ref=below.at[step, pl.ds(2, 1)],
                send_sem=halo_send.at[step, 3],
                recv_sem=halo_recv.at[step, 3],
                device_id=prev_id,
                device_id_type=MESH,
            ),
        ]

    up_set = [(rows - 2, 2), (rows - 1, 1), (rows - 1, 2)]
    down_set = [(0, 0), (0, 1), (1, 0)]
    inner_set = [
        (row, q)
        for row in range(rows)
        for q in range(3)
        if (row, q) not in up_set and (row, q) not in down_set
    ]

    def start_up(step):
        @pl.when(has_next)
        def _():
            for copy in up_copies(step):
                copy.start()

    def start_down(step):
        @pl.when(has_prev)
        def _():
            for copy in down_copies(step):
                copy.start()

    def basis_copy_of(slot, part):
        window = pl.ds(part * SEND_POINTS, SEND_POINTS)
        return pltpu.make_async_remote_copy(
            src_ref=packed.at[slot, window],
            dst_ref=arrived.at[slot, window],
            send_sem=basis_send.at[slot, part],
            recv_sem=basis_recv.at[slot, part],
            device_id=(wrapped(band + move_of(slot)), grid),
            device_id_type=MESH,
        )

    halves = band_count // 2
    parity = band % 2
    partner = wrapped(band + 1 - 2 * parity)
    has_partner = in_range(band + 1 - 2 * parity)
    level = band // 2
    rising = rounds * (halves - 1 - level) // halves
    falling = rounds * level // halves
    hops = jnp.where(has_partner, jnp.where(parity == 1, rising, falling), 0)
    passing = jnp.where(has_partner, jnp.where(parity == 1, falling, rising), 0)

    def hop_copy(slot, part):
        window = pl.ds(part * SEND_POINTS, SEND_POINTS)
        return pltpu.make_async_remote_copy(
            src_ref=packed.at[slot, window],
            dst_ref=transit.at[window],
            send_sem=basis_send.at[slot, part],
            recv_sem=hop_recv.at[part],
            device_id=(partner, grid),
            device_id_type=MESH,
        )

    def forward_copy(slot, part):
        window = pl.ds(part * SEND_POINTS, SEND_POINTS)
        return pltpu.make_async_remote_copy(
            src_ref=transit.at[window],
            dst_ref=arrived.at[slot, window],
            send_sem=hop_send.at[part],
            recv_sem=basis_recv.at[slot, part],
            device_id=(wrapped(band + 2 * move_of(slot)), grid),
            device_id_type=MESH,
        )

    def start_hop(part, carry):
        for slot in (1, 2):

            @pl.when((parity == slot - 1) & (part < hops))
            def _(slot=slot):
                hop_copy(slot, part).start()

        return carry

    def forward(part):
        for slot in (1, 2):

            @pl.when((parity == 2 - slot) & (part < passing))
            def _(slot=slot):
                hop_copy(slot, part).wait_recv()
                forward_copy(slot, part).start()

    def forward_part(part, carry):
        forward(part)
        return carry

    def start_round(part, slots):
        for slot in slots:
            direct = in_range(band + move_of(slot))
            if slot in (1, 2):
                direct = direct & jnp.logical_not((parity == slot - 1) & (part < hops))

            @pl.when(direct)
            def _(slot=slot):
                basis_copy_of(slot, part).start()

    x_copy.wait()
    for row, q in up_set:
        narrow[0, row, q] = x[row, q].astype(BF16)
    for row, q in down_set:
        narrow[0, row, q] = x[row, q].astype(BF16)
    for row, q in inner_set:
        narrow[0, row, q] = x[row, q].astype(BF16)

    @pl.when(jnp.logical_not(has_next))
    def _():
        below[...] = jnp.zeros_like(below)

    @pl.when(jnp.logical_not(has_prev))
    def _():
        above[...] = jnp.zeros_like(above)

    for copy in basis_copies:
        copy.wait()
    blocks_copy.wait()
    choices_copy.wait()
    firsts = []
    counts = []
    own_moves = []
    for d in range(local_domains):
        row_at = me * local_domains + d
        first = blocks_ref[0, row_at]
        firsts.append(first)
        live = jnp.int32(0)
        for k in range(blocks_ref.shape[0]):
            live = live + (blocks_ref[k, row_at] >= 0).astype(jnp.int32)
        counts.append(live)
        own_moves.append(lax.div(lax.div(first, jnp.int32(rows)), jnp.int32(grid_count)) - band)
    plans = []
    for slot in range(moves + 1):
        move = 0 if slot == moves else slot - REACH + slot // REACH
        chosen = jnp.int32(local_domains)
        offset = jnp.int32(0)
        count = jnp.int32(0)
        for d in range(local_domains):
            hit = own_moves[d] == move
            chosen = jnp.where(hit, d, chosen)
            offset = jnp.where(hit, lax.rem(firsts[d], jnp.int32(rows)), offset)
            count = jnp.where(hit, counts[d], count)
        places = []
        for k in range(rows):
            live = (k >= offset) & (k < offset + count)
            places.append(jnp.where(live, chosen * rows + k - offset, local_domains * rows))
        plans.append(places)

    def pack_part(part):
        window = pl.ds(pl.multiple_of(part * SEND_POINTS, SEND_POINTS), SEND_POINTS)
        for slot, places in enumerate(plans):
            for k, place in enumerate(places):
                value = basis[place, window]
                if slot == moves:
                    arrived[moves, window, k * width : (k + 1) * width] = value
                else:
                    packed[slot, window, k * width : (k + 1) * width] = value

    def pack_one(part, carry):
        pack_part(part)
        return carry

    lax.fori_loop(0, rounds, pack_one, 0)

    peers = jnp.int32(0)
    for live, _ in partners:
        peers = peers + live.astype(jnp.int32)
    pl.semaphore_wait(barrier, peers)
    start_up(0)
    start_down(0)

    at_edge = (grid == 0) | (grid == grid_count - 1)

    def start_near(part, carry):
        start_round(part, (1, 2))
        return carry

    def start_far(part, carry):
        start_round(part, (0, 3))
        return carry

    def start_all():
        lax.fori_loop(0, rounds, start_hop, 0)
        lax.fori_loop(0, rounds, start_far, 0)
        lax.fori_loop(0, rounds, start_near, 0)

    @pl.when(jnp.logical_not(at_edge))
    def _():
        start_all()

    def block_at(step, row, q):
        if 0 <= row < rows:
            return narrow[step, row, q]
        if row < 0:
            return above[step, {(-2, 2): 0, (-1, 1): 1, (-1, 2): 2}[(row, q)]]
        return below[step, {(0, 0): 0, (0, 1): 1, (1, 0): 2}[(row - rows, q)]]

    def update(step, row, q):
        gap = 2 - q
        column = row - gap
        total = None
        for middle in range(row - 2, column + 3):
            left_turned = middle > row
            left = block_at(step, max(row, middle), 2 - abs(row - middle))
            right_turned = middle < column
            right = block_at(step, max(column, middle), 2 - abs(column - middle))
            term = product(left, right, left_turned, right_turned)
            total = term if total is None else total + term
        chosen = jnp.broadcast_to(choices_ref[step], total.shape) == 1
        fresh = jnp.where(chosen, 2.0 * x[row, q] - total, total)
        x[row, q] = fresh
        narrow[step + 1, row, q] = fresh.astype(BF16)

    def purify(step, carry):
        @pl.when(has_next)
        def _():
            for copy in down_copies(step):
                copy.wait_recv()

        for row, q in up_set:
            update(step, row, q)

        @pl.when(step + 1 < ITERS)
        def _():
            start_up(step + 1)

        @pl.when(has_prev)
        def _():
            for copy in up_copies(step):
                copy.wait_recv()

        for row, q in down_set:
            update(step, row, q)

        @pl.when(step + 1 < ITERS)
        def _():
            start_down(step + 1)

        @pl.when(at_edge & (step == EDGE_STEP))
        def _():
            start_all()

        @pl.when(jnp.logical_not(at_edge))
        def _():
            lax.fori_loop(step * STEP_HOPS, (step + 1) * STEP_HOPS, forward_part, 0)

        for row, q in inner_set:
            update(step, row, q)
        return carry

    lax.fori_loop(0, ITERS, purify, 0)
    for k in range(rows):
        for gap in range(3):
            if k + gap < rows:
                tile = narrow[ITERS, k + gap, 2 - gap]
                tiles[k, gap * width : (gap + 1) * width] = tile if gap == 0 else tile * jnp.asarray(2.0, BF16)
    ham[...] = jnp.zeros_like(ham)
    factor = (rows * width) / points

    def domain_part(slot, part, publish):
        window = pl.ds(pl.multiple_of(part * PART_POINTS, PART_POINTS), PART_POINTS)

        def phi(first, last):
            return arrived[slot, window, first * width : last * width]

        summed = None
        for k in range(rows):
            last = min(k + 3, rows)
            applied = product(phi(k, last), tiles[k, : (last - k) * width], False, False)
            term = applied * phi(k, k + 1).astype(F32)
            summed = term if summed is None else summed + term
        potential = jnp.tanh(jnp.sum(summed, axis=1, keepdims=True))
        publish(jnp.transpose(jnp.broadcast_to(potential, (PART_POINTS, 128)))[:8])
        scale = factor * potential
        for k in range(rows):
            psi[:, k * width : (k + 1) * width] = (scale * phi(k, k + 1).astype(F32)).astype(BF16)
        for k in range(rows):
            first = max(k - 2, 0)
            found = product(psi[:, k * width : (k + 1) * width], phi(first, k + 1), True, False)
            for at in range(first, k + 1):
                ham[k, 2 - k + at] += found[:, (at - first) * width : (at - first + 1) * width]

    def own_part(part, carry):
        def publish(value):
            pot_in[moves, part] = value

        domain_part(moves, part, publish)
        return carry

    lax.fori_loop(0, parts, own_part, 0)

    def pot_copy(slot, part):
        return pltpu.make_async_remote_copy(
            src_ref=pot_out.at[slot, part],
            dst_ref=pot_in.at[slot, part],
            send_sem=pot_send.at[slot, part],
            recv_sem=pot_recv.at[slot, part],
            device_id=(wrapped(band - move_of(slot)), grid),
            device_id_type=MESH,
        )

    forwarded = jnp.where(at_edge, 0, ITERS * STEP_HOPS)

    def other_part(index, carry):
        reached = jnp.minimum(forwarded + index * STEP_HOPS, rounds)
        lax.fori_loop(reached, jnp.minimum(reached + STEP_HOPS, rounds), forward_part, 0)

        part = index // moves
        slot = (index % moves) * (moves - 1) % moves

        @pl.when(in_range(band - move_of(slot)))
        def _():
            for piece in range(per_part):
                basis_copy_of(slot, part * per_part + piece).wait_recv()

            def publish(value):
                pot_out[slot, part] = value
                pot_copy(slot, part).start()

            domain_part(slot, part, publish)

        return carry

    lax.fori_loop(0, parts * moves, other_part, 0)

    def settle_halo(step, carry):
        @pl.when(has_next)
        def _():
            for copy in up_copies(step):
                copy.wait_send()

        @pl.when(has_prev)
        def _():
            for copy in down_copies(step):
                copy.wait_send()

        return carry

    lax.fori_loop(0, ITERS, settle_halo, 0)

    def settle_basis(index, carry):
        slot = index // rounds

        @pl.when(in_range(band + move_of(slot)))
        def _():
            basis_copy_of(slot, index % rounds).wait_send()

        return carry

    lax.fori_loop(0, moves * rounds, settle_basis, 0)

    def settle_hop(part, carry):
        for slot in (1, 2):

            @pl.when((parity == 2 - slot) & (part < passing))
            def _(slot=slot):
                forward_copy(slot, part).wait_send()

        return carry

    lax.fori_loop(0, rounds, settle_hop, 0)

    def settle_pot(index, carry):
        slot = index // parts
        part = index % parts

        @pl.when(in_range(band - move_of(slot)))
        def _():
            pot_copy(slot, part).wait_send()

        @pl.when(in_range(band + move_of(slot)))
        def _():
            pot_copy(slot, part).wait_recv()

        return carry

    lax.fori_loop(0, moves * parts, settle_pot, 0)
    for d in range(local_domains):
        chosen = jnp.int32(moves)
        for slot in range(moves):
            chosen = jnp.where(own_moves[d] == move_of(slot), slot, chosen)
        for part in range(parts):
            window = slice(part * PART_POINTS, (part + 1) * PART_POINTS)
            potential_ref[d : d + 1, window] = pot_in[chosen, part][:1]


def write_out(*refs):
    count = len(refs) // 2
    sem = refs[-1]
    copies = [pltpu.make_async_copy(refs[at], refs[count + at], sem.at[at]) for at in range(count)]
    for copy in copies:
        copy.start()
    for copy in copies:
        copy.wait()


def solution(mesh):
    band_count = mesh.shape["band"]
    grid_count = mesh.shape["grid"]

    def body(x_initial, sp2_choices, domain_blocks, basis_values):
        rows, gaps, width, _ = x_initial.shape
        local_domains, points, columns = basis_values.shape
        moves = 2 * REACH
        rounds = points // SEND_POINTS
        parts = points // PART_POINTS
        in_hbm = pl.BlockSpec(memory_space=pltpu.HBM)
        anywhere = pl.BlockSpec(memory_space=pl.ANY)
        in_vmem = pl.BlockSpec(memory_space=pltpu.VMEM)
        results = pl.pallas_call(
            functools.partial(kernel, band_count, grid_count),
            out_shape=(
                jax.ShapeDtypeStruct(x_initial.shape, F32),
                jax.ShapeDtypeStruct(x_initial.shape, F32),
                jax.ShapeDtypeStruct((local_domains, points), F32),
            ),
            in_specs=[in_hbm, in_hbm, anywhere, anywhere],
            out_specs=(in_vmem, in_vmem, in_vmem),
            scratch_shapes=[
                pltpu.VMEM((local_domains * rows + 1, points, width), BF16),
                pltpu.VMEM((ITERS + 1,) + x_initial.shape, BF16),
                pltpu.VMEM((rows, 3 * width, width), BF16),
                pltpu.VMEM((ITERS, 3, width, width), BF16),
                pltpu.VMEM((ITERS, 3, width, width), BF16),
                pltpu.VMEM((moves, points, columns), BF16),
                pltpu.VMEM((moves + 1, points, columns), BF16),
                pltpu.VMEM((points, columns), BF16),
                pltpu.VMEM((PART_POINTS, columns), BF16),
                pltpu.VMEM((moves + 1, parts, 8, PART_POINTS), F32),
                pltpu.VMEM((moves, parts, 8, PART_POINTS), F32),
                pltpu.SMEM(domain_blocks.shape[::-1], jnp.int32),
                pltpu.SMEM(sp2_choices.shape, jnp.int32),
                pltpu.SemaphoreType.DMA((3,)),
                pltpu.SemaphoreType.DMA((local_domains * rows,)),
                pltpu.SemaphoreType.DMA((ITERS, 4)),
                pltpu.SemaphoreType.DMA((ITERS, 4)),
                pltpu.SemaphoreType.DMA((moves, rounds)),
                pltpu.SemaphoreType.DMA((moves, rounds)),
                pltpu.SemaphoreType.DMA((rounds,)),
                pltpu.SemaphoreType.DMA((rounds,)),
                pltpu.SemaphoreType.DMA((moves, parts)),
                pltpu.SemaphoreType.DMA((moves, parts)),
            ],
            compiler_params=pltpu.CompilerParams(
                collective_id=0, has_side_effects=True, vmem_limit_bytes=VMEM_LIMIT
            ),
        )(domain_blocks.T, sp2_choices, x_initial, basis_values)
        return pl.pallas_call(
            write_out,
            out_shape=tuple(jax.ShapeDtypeStruct(held.shape, held.dtype) for held in results),
            in_specs=[in_vmem] * len(results),
            out_specs=(in_hbm,) * len(results),
            scratch_shapes=[pltpu.SemaphoreType.DMA((len(results),))],
            compiler_params=pltpu.CompilerParams(vmem_limit_bytes=SMALL_LIMIT),
        )(*results)

    placed = (P(("band", "grid"), None, None, None), P(), P(), P(("band", "grid"), None, None))
    return jax.shard_map(
        body,
        mesh=mesh,
        in_specs=placed,
        out_specs=(
            P(("band", "grid"), None, None, None),
            P(("band", "grid"), None, None, None),
            P(("band", "grid"), None),
        ),
        check_vma=False,
    )
```

```python
import functools

import jax
import jax.numpy as jnp
from jax import lax
from jax.experimental import pallas as pl
from jax.experimental.pallas import tpu as pltpu
from jax.sharding import PartitionSpec as P

REACH = 2
ITERS = 4
SEND_POINTS = 64
PART_POINTS = 256
EDGE_STEP = ITERS - 2
STEP_HOPS = 3
VMEM_LIMIT = 48000000
SMALL_LIMIT = 1000000
MESH = pl.DeviceIdType.MESH
F32 = jnp.float32
BF16 = jnp.bfloat16


def product(left, right, left_turned, right_turned):
    dims = (((0 if left_turned else 1,), (1 if right_turned else 0,)), ((), ()))
    return lax.dot_general(left, right, dims, preferred_element_type=F32)


def kernel(
    band_count,
    grid_count,
    blocks_hbm,
    choices_hbm,
    x_hbm,
    basis_hbm,
    x,
    ham,
    potential_ref,
    basis,
    narrow,
    tiles,
    above,
    below,
    packed,
    arrived,
    transit,
    psi,
    pot_in,
    pot_out,
    blocks_ref,
    choices_ref,
    local_sem,
    basis_sem,
    halo_send,
    halo_recv,
    basis_send,
    basis_recv,
    hop_send,
    hop_recv,
    pot_send,
    pot_recv,
):
    rows, _, width, _ = x.shape
    _, points, _ = basis_hbm.shape
    local_domains = basis_hbm.shape[0]
    rounds = points // SEND_POINTS
    parts = points // PART_POINTS
    per_part = PART_POINTS // SEND_POINTS
    moves = 2 * REACH
    band = lax.axis_index("band")
    grid = lax.axis_index("grid")
    me = band * grid_count + grid
    device_count = band_count * grid_count
    has_next = me + 1 < device_count
    has_prev = me > 0
    following = (me + 1) % device_count
    preceding = (me + device_count - 1) % device_count
    next_id = (following // grid_count, following % grid_count)
    prev_id = (preceding // grid_count, preceding % grid_count)

    def move_of(slot):
        return slot - REACH + slot // REACH

    def in_range(at_band):
        return (at_band >= 0) & (at_band < band_count)

    def wrapped(at_band):
        return (at_band + band_count) % band_count

    blocks_copy = pltpu.make_async_copy(blocks_hbm, blocks_ref, local_sem.at[1])
    blocks_copy.start()
    choices_copy = pltpu.make_async_copy(choices_hbm, choices_ref, local_sem.at[2])
    choices_copy.start()
    x_copy = pltpu.make_async_copy(x_hbm, x, local_sem.at[0])
    x_copy.start()
    basis_copies = []
    for d in range(local_domains):
        for k in range(rows):
            basis_copies.append(
                pltpu.make_async_copy(
                    basis_hbm.at[d, :, pl.ds(k * width, width)],
                    basis.at[d * rows + k],
                    basis_sem.at[d * rows + k],
                )
            )
    for copy in basis_copies:
        copy.start()
    pot_in[...] = jnp.zeros_like(pot_in)
    basis[local_domains * rows] = jnp.zeros((points, width), BF16)

    barrier = pltpu.get_barrier_semaphore()
    partners = [(has_next, next_id), (has_prev, prev_id)]
    for slot in range(moves):
        other = band + move_of(slot)
        partners.append((in_range(other), (wrapped(other), grid)))
    for live, target in partners:

        @pl.when(live)
        def _(target=target):
            pl.semaphore_signal(barrier, inc=1, device_id=target, device_id_type=MESH)

    def up_copies(step):
        return [
            pltpu.make_async_remote_copy(
                src_ref=narrow.at[step, rows - 2, pl.ds(2, 1)],
                dst_ref=above.at[step, pl.ds(0, 1)],
                send_sem=halo_send.at[step, 0],
                recv_sem=halo_recv.at[step, 0],
                device_id=next_id,
                device_id_type=MESH,
            ),
            pltpu.make_async_remote_copy(
                src_ref=narrow.at[step, rows - 1, pl.ds(1, 2)],
                dst_ref=above.at[step, pl.ds(1, 2)],
                send_sem=halo_send.at[step, 1],
                recv_sem=halo_recv.at[step, 1],
                device_id=next_id,
                device_id_type=MESH,
            ),
        ]

    def down_copies(step):
        return [
            pltpu.make_async_remote_copy(
                src_ref=narrow.at[step, 0, pl.ds(0, 2)],
                dst_ref=below.at[step, pl.ds(0, 2)],
                send_sem=halo_send.at[step, 2],
                recv_sem=halo_recv.at[step, 2],
                device_id=prev_id,
                device_id_type=MESH,
            ),
            pltpu.make_async_remote_copy(
                src_ref=narrow.at[step, 1, pl.ds(0, 1)],
                dst_ref=below.at[step, pl.ds(2, 1)],
                send_sem=halo_send.at[step, 3],
                recv_sem=halo_recv.at[step, 3],
                device_id=prev_id,
                device_id_type=MESH,
            ),
        ]

    up_set = [(rows - 2, 2), (rows - 1, 1), (rows - 1, 2)]
    down_set = [(0, 0), (0, 1), (1, 0)]
    inner_set = [
        (row, q)
        for row in range(rows)
        for q in range(3)
        if (row, q) not in up_set and (row, q) not in down_set
    ]

    def start_up(step):
        @pl.when(has_next)
        def _():
            for copy in up_copies(step):
                copy.start()

    def start_down(step):
        @pl.when(has_prev)
        def _():
            for copy in down_copies(step):
                copy.start()

    def basis_copy_of(slot, part):
        window = pl.ds(part * SEND_POINTS, SEND_POINTS)
        return pltpu.make_async_remote_copy(
            src_ref=packed.at[slot, window],
            dst_ref=arrived.at[slot, window],
            send_sem=basis_send.at[slot, part],
            recv_sem=basis_recv.at[slot, part],
            device_id=(wrapped(band + move_of(slot)), grid),
            device_id_type=MESH,
        )

    halves = band_count // 2
    parity = band % 2
    partner = wrapped(band + 1 - 2 * parity)
    has_partner = in_range(band + 1 - 2 * parity)
    level = band // 2
    rising = rounds * (halves - 1 - level) // halves
    falling = rounds * level // halves
    outer = (grid == 0) | (grid == grid_count - 1)
    rising = jnp.where(outer, jnp.maximum(rising - 1, 0), jnp.where(level + 1 < halves, rising + 1, rising))
    falling = jnp.where(outer, jnp.maximum(falling - 1, 0), jnp.where(level > 0, falling + 1, falling))
    hops = jnp.where(has_partner, jnp.where(parity == 1, rising, falling), 0)
    passing = jnp.where(has_partner, jnp.where(parity == 1, falling, rising), 0)

    def hop_copy(slot, part):
        window = pl.ds(part * SEND_POINTS, SEND_POINTS)
        return pltpu.make_async_remote_copy(
            src_ref=packed.at[slot, window],
            dst_ref=transit.at[window],
            send_sem=basis_send.at[slot, part],
            recv_sem=hop_recv.at[part],
            device_id=(partner, grid),
            device_id_type=MESH,
        )

    def forward_copy(slot, part):
        window = pl.ds(part * SEND_POINTS, SEND_POINTS)
        return pltpu.make_async_remote_copy(
            src_ref=transit.at[window],
            dst_ref=arrived.at[slot, window],
            send_sem=hop_send.at[part],
            recv_sem=basis_recv.at[slot, part],
            device_id=(wrapped(band + 2 * move_of(slot)), grid),
            device_id_type=MESH,
        )

    def start_hop(part, carry):
        for slot in (1, 2):

            @pl.when((parity == slot - 1) & (part < hops))
            def _(slot=slot):
                hop_copy(slot, part).start()

        return carry

    def forward(part):
        for slot in (1, 2):

            @pl.when((parity == 2 - slot) & (part < passing))
            def _(slot=slot):
                hop_copy(slot, part).wait_recv()
                forward_copy(slot, part).start()

    def forward_part(part, carry):
        forward(part)
        return carry

    def start_round(part, slots):
        for slot in slots:
            direct = in_range(band + move_of(slot))
            if slot in (1, 2):
                direct = direct & jnp.logical_not((parity == slot - 1) & (part < hops))

            @pl.when(direct)
            def _(slot=slot):
                basis_copy_of(slot, part).start()

    x_copy.wait()
    for row, q in up_set:
        narrow[0, row, q] = x[row, q].astype(BF16)
    for row, q in down_set:
        narrow[0, row, q] = x[row, q].astype(BF16)
    for row, q in inner_set:
        narrow[0, row, q] = x[row, q].astype(BF16)

    @pl.when(jnp.logical_not(has_next))
    def _():
        below[...] = jnp.zeros_like(below)

    @pl.when(jnp.logical_not(has_prev))
    def _():
        above[...] = jnp.zeros_like(above)

    for copy in basis_copies:
        copy.wait()
    blocks_copy.wait()
    choices_copy.wait()
    firsts = []
    counts = []
    own_moves = []
    for d in range(local_domains):
        row_at = me * local_domains + d
        first = blocks_ref[0, row_at]
        firsts.append(first)
        live = jnp.int32(0)
        for k in range(blocks_ref.shape[0]):
            live = live + (blocks_ref[k, row_at] >= 0).astype(jnp.int32)
        counts.append(live)
        own_moves.append(lax.div(lax.div(first, jnp.int32(rows)), jnp.int32(grid_count)) - band)
    plans = []
    for slot in range(moves + 1):
        move = 0 if slot == moves else slot - REACH + slot // REACH
        chosen = jnp.int32(local_domains)
        offset = jnp.int32(0)
        count = jnp.int32(0)
        for d in range(local_domains):
            hit = own_moves[d] == move
            chosen = jnp.where(hit, d, chosen)
            offset = jnp.where(hit, lax.rem(firsts[d], jnp.int32(rows)), offset)
            count = jnp.where(hit, counts[d], count)
        places = []
        for k in range(rows):
            live = (k >= offset) & (k < offset + count)
            places.append(jnp.where(live, chosen * rows + k - offset, local_domains * rows))
        plans.append(places)

    def pack_part(part):
        window = pl.ds(pl.multiple_of(part * SEND_POINTS, SEND_POINTS), SEND_POINTS)
        for slot, places in enumerate(plans):
            for k, place in enumerate(places):
                value = basis[place, window]
                if slot == moves:
                    arrived[moves, window, k * width : (k + 1) * width] = value
                else:
                    packed[slot, window, k * width : (k + 1) * width] = value

    def pack_one(part, carry):
        pack_part(part)
        return carry

    lax.fori_loop(0, rounds, pack_one, 0)

    peers = jnp.int32(0)
    for live, _ in partners:
        peers = peers + live.astype(jnp.int32)
    pl.semaphore_wait(barrier, peers)
    start_up(0)
    start_down(0)

    at_edge = (grid == 0) | (grid == grid_count - 1)

    def start_near(part, carry):
        start_round(part, (1, 2))
        return carry

    def start_far(part, carry):
        start_round(part, (0, 3))
        return carry

    def start_all():
        lax.fori_loop(0, rounds, start_hop, 0)
        lax.fori_loop(0, rounds, start_far, 0)
        lax.fori_loop(0, rounds, start_near, 0)

    @pl.when(jnp.logical_not(at_edge))
    def _():
        start_all()

    def block_at(step, row, q):
        if 0 <= row < rows:
            return narrow[step, row, q]
        if row < 0:
            return above[step, {(-2, 2): 0, (-1, 1): 1, (-1, 2): 2}[(row, q)]]
        return below[step, {(0, 0): 0, (0, 1): 1, (1, 0): 2}[(row - rows, q)]]

    def update(step, row, q):
        gap = 2 - q
        column = row - gap
        total = None
        for middle in range(row - 2, column + 3):
            left_turned = middle > row
            left = block_at(step, max(row, middle), 2 - abs(row - middle))
            right_turned = middle < column
            right = block_at(step, max(column, middle), 2 - abs(column - middle))
            term = product(left, right, left_turned, right_turned)
            total = term if total is None else total + term
        chosen = jnp.broadcast_to(choices_ref[step], total.shape) == 1
        fresh = jnp.where(chosen, 2.0 * x[row, q] - total, total)
        x[row, q] = fresh
        narrow[step + 1, row, q] = fresh.astype(BF16)

    def purify(step, carry):
        @pl.when(has_next)
        def _():
            for copy in down_copies(step):
                copy.wait_recv()

        for row, q in up_set:
            update(step, row, q)

        @pl.when(step + 1 < ITERS)
        def _():
            start_up(step + 1)

        @pl.when(has_prev)
        def _():
            for copy in up_copies(step):
                copy.wait_recv()

        for row, q in down_set:
            update(step, row, q)

        @pl.when(step + 1 < ITERS)
        def _():
            start_down(step + 1)

        @pl.when(at_edge & (step == EDGE_STEP))
        def _():
            start_all()

        @pl.when(jnp.logical_not(at_edge))
        def _():
            lax.fori_loop(step * STEP_HOPS, (step + 1) * STEP_HOPS, forward_part, 0)

        for row, q in inner_set:
            update(step, row, q)

        @pl.when(at_edge & (step == ITERS - 1))
        def _():
            lax.fori_loop(0, STEP_HOPS, forward_part, 0)

        return carry

    lax.fori_loop(0, ITERS, purify, 0)
    for k in range(rows):
        for gap in range(3):
            if k + gap < rows:
                tile = narrow[ITERS, k + gap, 2 - gap]
                tiles[k, gap * width : (gap + 1) * width] = tile if gap == 0 else tile * jnp.asarray(2.0, BF16)
    ham[...] = jnp.zeros_like(ham)
    factor = (rows * width) / points

    def domain_part(slot, part, publish):
        window = pl.ds(pl.multiple_of(part * PART_POINTS, PART_POINTS), PART_POINTS)

        def phi(first, last):
            return arrived[slot, window, first * width : last * width]

        summed = None
        for k in range(rows):
            last = min(k + 3, rows)
            applied = product(phi(k, last), tiles[k, : (last - k) * width], False, False)
            term = applied * phi(k, k + 1).astype(F32)
            summed = term if summed is None else summed + term
        potential = jnp.tanh(jnp.sum(summed, axis=1, keepdims=True))
        publish(jnp.transpose(jnp.broadcast_to(potential, (PART_POINTS, 128)))[:8])
        scale = factor * potential
        for k in range(rows):
            psi[:, k * width : (k + 1) * width] = (scale * phi(k, k + 1).astype(F32)).astype(BF16)
        for k in range(rows):
            first = max(k - 2, 0)
            found = product(psi[:, k * width : (k + 1) * width], phi(first, k + 1), True, False)
            for at in range(first, k + 1):
                ham[k, 2 - k + at] += found[:, (at - first) * width : (at - first + 1) * width]

    def own_part(part, carry):
        def publish(value):
            pot_in[moves, part] = value

        domain_part(moves, part, publish)
        return carry

    lax.fori_loop(0, parts, own_part, 0)

    def pot_copy(slot, part):
        return pltpu.make_async_remote_copy(
            src_ref=pot_out.at[slot, part],
            dst_ref=pot_in.at[slot, part],
            send_sem=pot_send.at[slot, part],
            recv_sem=pot_recv.at[slot, part],
            device_id=(wrapped(band - move_of(slot)), grid),
            device_id_type=MESH,
        )

    forwarded = jnp.where(at_edge, STEP_HOPS, ITERS * STEP_HOPS)

    def other_part(index, carry):
        reached = jnp.minimum(forwarded + index * STEP_HOPS, rounds)
        lax.fori_loop(reached, jnp.minimum(reached + STEP_HOPS, rounds), forward_part, 0)

        part = index // moves
        slot = (index % moves) * (moves - 1) % moves

        @pl.when(in_range(band - move_of(slot)))
        def _():
            for piece in range(per_part):
                basis_copy_of(slot, part * per_part + piece).wait_recv()

            def publish(value):
                pot_out[slot, part] = value
                pot_copy(slot, part).start()

            domain_part(slot, part, publish)

        return carry

    lax.fori_loop(0, parts * moves, other_part, 0)

    def settle_halo(step, carry):
        @pl.when(has_next)
        def _():
            for copy in up_copies(step):
                copy.wait_send()

        @pl.when(has_prev)
        def _():
            for copy in down_copies(step):
                copy.wait_send()

        return carry

    lax.fori_loop(0, ITERS, settle_halo, 0)

    def settle_basis(index, carry):
        slot = index // rounds

        @pl.when(in_range(band + move_of(slot)))
        def _():
            basis_copy_of(slot, index % rounds).wait_send()

        return carry

    lax.fori_loop(0, moves * rounds, settle_basis, 0)

    def settle_hop(part, carry):
        for slot in (1, 2):

            @pl.when((parity == 2 - slot) & (part < passing))
            def _(slot=slot):
                forward_copy(slot, part).wait_send()

        return carry

    lax.fori_loop(0, rounds, settle_hop, 0)

    def settle_pot(index, carry):
        slot = index // parts
        part = index % parts

        @pl.when(in_range(band - move_of(slot)))
        def _():
            pot_copy(slot, part).wait_send()

        @pl.when(in_range(band + move_of(slot)))
        def _():
            pot_copy(slot, part).wait_recv()

        return carry

    lax.fori_loop(0, moves * parts, settle_pot, 0)
    for d in range(local_domains):
        chosen = jnp.int32(moves)
        for slot in range(moves):
            chosen = jnp.where(own_moves[d] == move_of(slot), slot, chosen)
        for part in range(parts):
            window = slice(part * PART_POINTS, (part + 1) * PART_POINTS)
            potential_ref[d : d + 1, window] = pot_in[chosen, part][:1]


def write_out(*refs):
    count = len(refs) // 2
    sem = refs[-1]
    copies = [pltpu.make_async_copy(refs[at], refs[count + at], sem.at[at]) for at in range(count)]
    for copy in copies:
        copy.start()
    for copy in copies:
        copy.wait()


def solution(mesh):
    band_count = mesh.shape["band"]
    grid_count = mesh.shape["grid"]

    def body(x_initial, sp2_choices, domain_blocks, basis_values):
        rows, gaps, width, _ = x_initial.shape
        local_domains, points, columns = basis_values.shape
        moves = 2 * REACH
        rounds = points // SEND_POINTS
        parts = points // PART_POINTS
        in_hbm = pl.BlockSpec(memory_space=pltpu.HBM)
        anywhere = pl.BlockSpec(memory_space=pl.ANY)
        in_vmem = pl.BlockSpec(memory_space=pltpu.VMEM)
        results = pl.pallas_call(
            functools.partial(kernel, band_count, grid_count),
            out_shape=(
                jax.ShapeDtypeStruct(x_initial.shape, F32),
                jax.ShapeDtypeStruct(x_initial.shape, F32),
                jax.ShapeDtypeStruct((local_domains, points), F32),
            ),
            in_specs=[in_hbm, in_hbm, anywhere, anywhere],
            out_specs=(in_vmem, in_vmem, in_vmem),
            scratch_shapes=[
                pltpu.VMEM((local_domains * rows + 1, points, width), BF16),
                pltpu.VMEM((ITERS + 1,) + x_initial.shape, BF16),
                pltpu.VMEM((rows, 3 * width, width), BF16),
                pltpu.VMEM((ITERS, 3, width, width), BF16),
                pltpu.VMEM((ITERS, 3, width, width), BF16),
                pltpu.VMEM((moves, points, columns), BF16),
                pltpu.VMEM((moves + 1, points, columns), BF16),
                pltpu.VMEM((points, columns), BF16),
                pltpu.VMEM((PART_POINTS, columns), BF16),
                pltpu.VMEM((moves + 1, parts, 8, PART_POINTS), F32),
                pltpu.VMEM((moves, parts, 8, PART_POINTS), F32),
                pltpu.SMEM(domain_blocks.shape[::-1], jnp.int32),
                pltpu.SMEM(sp2_choices.shape, jnp.int32),
                pltpu.SemaphoreType.DMA((3,)),
                pltpu.SemaphoreType.DMA((local_domains * rows,)),
                pltpu.SemaphoreType.DMA((ITERS, 4)),
                pltpu.SemaphoreType.DMA((ITERS, 4)),
                pltpu.SemaphoreType.DMA((moves, rounds)),
                pltpu.SemaphoreType.DMA((moves, rounds)),
                pltpu.SemaphoreType.DMA((rounds,)),
                pltpu.SemaphoreType.DMA((rounds,)),
                pltpu.SemaphoreType.DMA((moves, parts)),
                pltpu.SemaphoreType.DMA((moves, parts)),
            ],
            compiler_params=pltpu.CompilerParams(
                collective_id=0, has_side_effects=True, vmem_limit_bytes=VMEM_LIMIT
            ),
        )(domain_blocks.T, sp2_choices, x_initial, basis_values)
        return pl.pallas_call(
            write_out,
            out_shape=tuple(jax.ShapeDtypeStruct(held.shape, held.dtype) for held in results),
            in_specs=[in_vmem] * len(results),
            out_specs=(in_hbm,) * len(results),
            scratch_shapes=[pltpu.SemaphoreType.DMA((len(results),))],
            compiler_params=pltpu.CompilerParams(vmem_limit_bytes=SMALL_LIMIT),
        )(*results)

    placed = (P(("band", "grid"), None, None, None), P(), P(), P(("band", "grid"), None, None))
    return jax.shard_map(
        body,
        mesh=mesh,
        in_specs=placed,
        out_specs=(
            P(("band", "grid"), None, None, None),
            P(("band", "grid"), None, None, None),
            P(("band", "grid"), None),
        ),
        check_vma=False,
    )
```
